512 devices in a mesh: layer: 16 (over z), row: 8 (over x, core), col: 4 (over y).
Axes of the slice: x: 4, y: 4, z: 16, core: 2. Of those that a mesh axis runs over, the one named last changes fastest.
Arguments:
- density: float32 [4096, 4096], P(('row', 'col'), 'layer'), as said below
- pattern: int32 [32, 32], replicated, may hold values from 0 to 1, as said below
Outputs:
- purified: float32 [4096, 4096], P(('row', 'col'), 'layer')
The draws below stay inside these ranges and needn't reach their ends.
Inputs may be any that keep to these rules, and one draw needn't show every extreme that they name: pattern is symmetric, its diagonal is all ones. density is symmetric.
All inputs are finite; a program needn't handle non-finite values.
Results may differ from the reference program's by a relative error of at most 0.00013.
Values sent between devices are 32-bit elements; how exact they have to be, the bound alone decides.
No kernel may reach another device: no remote copies, remote signals or barrier semaphores. Data moves between devices by JAX's collectives and lax.ppermute only.
A program may use at most 64 MiB of HBM per device.

```python
import jax
import jax.numpy as jnp
from jax import lax

TILE = 128
TILES = 32
ORDER = 4096


def draw_density(key, part):
    first = jax.random.fold_in(key, 11)
    second = jax.random.fold_in(key, 12)
    noise = jax.random.normal(first, (ORDER, ORDER), jnp.float32)
    spread = 0.3 / jnp.sqrt(ORDER / 2.0)
    symmetric = (noise + noise.T) * (spread / jnp.sqrt(2.0))
    diagonal = jax.random.uniform(second, (ORDER,), jnp.float32, 0.2, 0.8)
    return symmetric + jnp.diag(diagonal)


def draw_pattern(key, part):
    scores = jax.random.randint(jax.random.fold_in(key, 21), (TILES, TILES), 0, 100)
    index = jnp.arange(TILES, dtype=jnp.int32)
    first = index[:, None]
    second = index[None, :]
    bound = 15 + 70 * (first + second) // (2 * (TILES - 1))
    upper = (scores < bound).astype(jnp.int32)
    both = jnp.where(first <= second, upper, upper.T)
    both = jnp.where(first == second, 1, both)
    corner = (first == 0) & (second == TILES - 1) | (first == TILES - 1) & (second == 0)
    return jnp.where(corner, 0, both).astype(jnp.int32)


def setup_inputs(seed: int = 0) -> dict:
    splits = jax.random.split(jax.random.key(seed), 3)
    density = draw_density(jax.random.fold_in(splits[2], 71), 0)
    pattern = draw_pattern(jax.random.fold_in(splits[2], 71), 0)
    return dict(density=density, pattern=pattern)


def reference(density, pattern):
    keep = pattern.astype(density.dtype)
    mask = jnp.repeat(jnp.repeat(keep, TILE, axis=0), TILE, axis=1)
    masked = density * mask
    square = jnp.dot(masked, masked, precision=lax.Precision.HIGHEST, preferred_element_type=jnp.float32)
    cube = jnp.dot(square, masked, precision=lax.Precision.HIGHEST, preferred_element_type=jnp.float32)
    return 3.0 * square - 2.0 * cube
```

```python
import jax
import jax.numpy as jnp
from jax import lax
from jax.experimental import pallas as pl
from jax.experimental.pallas import tpu as pltpu
from jax.sharding import Mesh
from jax.sharding import PartitionSpec as P

TILE = 128
LAYERS = 16
HALF = 8


def split(value):
    high = value.astype(jnp.bfloat16)
    low = (value - high.astype(jnp.float32)).astype(jnp.bfloat16)
    return high, low


def product_body(place, lefts, mine_ref, other_ref, left_scratch):
    pair, parity, core = place[0], place[1], place[2]
    for distance, left_ref in lefts:
        slot = lax.rem(pair + (distance + HALF), HALF)
        high, low = split(left_ref[...])
        left_scratch[slot, 0:TILE, :] = high
        left_scratch[slot, TILE : 2 * TILE, :] = low
    totals = []
    for side in range(2):
        total = jnp.zeros((TILE, 2 * TILE), jnp.float32)
        which = parity if side == 0 else 1 - parity
        for block_ref, core_index in ((mine_ref, core), (other_ref, 1 - core)):
            for x in range(4):
                block = block_ref[pl.ds(4 * x + 2 * which, 2)].reshape(2 * TILE, 2 * TILE)
                high, low = split(block)
                left = left_scratch[2 * x + core_index]
                both = jnp.dot(left, high, preferred_element_type=jnp.float32)
                cross = jnp.dot(left[:TILE], low, preferred_element_type=jnp.float32)
                total += both[:TILE] + (both[TILE:] + cross)
        totals.append(total)
    return totals


DISTANCES = (0, -1, 1, -2, 2, -3, 3, -4)


def first_kernel(place, *refs):
    lefts = list(zip(DISTANCES, refs[:HALF], strict=True))
    mine_ref, other_ref, own_out, other_out, scratch = refs[HALF:]
    own, other = product_body(place, lefts, mine_ref, other_ref, scratch)
    own_out[...] = own
    other_out[...] = other


def second_kernel(place, *refs):
    lefts = list(zip(DISTANCES, refs[:HALF], strict=True))
    mine_ref, other_ref, own_in, other_in, own_out, other_out, scratch = refs[HALF:]
    own, other = product_body(place, lefts, mine_ref, other_ref, scratch)
    own_out[...] = 3.0 * own_in[...] - 2.0 * own
    other_out[...] = 3.0 * other_in[...] - 2.0 * other


def call(kernel, place, operands):
    vmem = pl.BlockSpec(memory_space=pltpu.VMEM)
    out = jax.ShapeDtypeStruct((TILE, 2 * TILE), jnp.float32)
    return pl.pallas_call(
        kernel,
        out_shape=(out, out),
        in_specs=[pl.BlockSpec(memory_space=pltpu.SMEM)] + [vmem] * len(operands),
        out_specs=(vmem, vmem),
        scratch_shapes=[pltpu.VMEM((HALF, 2 * TILE, 2 * TILE), jnp.bfloat16)],
        cost_estimate=pl.CostEstimate(
            flops=6 * 128 * 2048 * 512, bytes_accessed=6 << 20, transcendentals=0
        ),
    )(place, *operands)


def ring(block):
    up = [(z, (z + 2) % LAYERS) for z in range(LAYERS)]
    down = [(z, (z - 2) % LAYERS) for z in range(LAYERS)]
    blocks = [block]
    ahead = behind = block
    for _ in range(3):
        ahead = lax.ppermute(ahead, "z", up)
        behind = lax.ppermute(behind, "z", down)
        blocks += [ahead, behind]
    blocks.append(lax.ppermute(ahead, "z", up))
    return blocks


def on_device(density, pattern):
    layer, row, col = lax.axis_index("z"), lax.axis_index(("x", "c", "y")), lax.axis_index("y")
    parity = layer % 2
    keep = lax.dynamic_slice(pattern, (row, 2 * layer), (1, 2)).astype(jnp.float32)
    column = lax.broadcasted_iota(jnp.int32, density.shape, 1)
    masked = density * jnp.where(column < TILE, keep[0, 0], keep[0, 1])

    swap = [
        (4 * z + y, 4 * (z ^ 1) + (y ^ 2))
        for z in range(LAYERS)
        for y in range(4)
        if z % 2 != y // 2
    ]
    moved = lax.ppermute(masked, ("z", "y"), swap)
    panel = jnp.where(col // 2 == parity, masked, moved)
    mine = lax.all_to_all(
        jnp.broadcast_to(panel[None], (16, TILE, 2 * TILE)), ("x", "y"), 0, 0
    )
    other = lax.ppermute(mine, "c", [(0, 1), (1, 0)])

    pairs = [(z, z ^ 1) for z in range(LAYERS)]
    place = jnp.stack([layer // 2, parity, lax.axis_index("c")]).astype(jnp.int32)
    own_square, other_square = call(first_kernel, place, [*ring(masked), mine, other])
    square = own_square + lax.ppermute(other_square, "z", pairs)
    own, away = call(
        second_kernel, place, [*ring(square), mine, other, own_square, other_square]
    )
    return own + lax.ppermute(away, "z", pairs)


def solution(mesh):
    split_mesh = Mesh(mesh.devices.reshape(LAYERS, 4, 2, 4), ("z", "x", "c", "y"))
    return jax.shard_map(
        on_device,
        mesh=split_mesh,
        in_specs=(P(("x", "c", "y"), "z"), P()),
        out_specs=P(("x", "c", "y"), "z"),
        check_vma=False,
    )
```

```python
import jax
import jax.numpy as jnp
from jax import lax
from jax.experimental import pallas as pl
from jax.experimental.pallas import tpu as pltpu
from jax.sharding import Mesh
from jax.sharding import PartitionSpec as P


TILE = 128
LAYERS = 16
HALF = 8
DISTANCES = (0, -1, 1, -2, 2, -3, 3, -4)


VMEM = pl.BlockSpec(memory_space=pltpu.VMEM)


def shape(*dims):
    return jax.ShapeDtypeStruct(dims, jnp.float32)


def split(value):
    high = value.astype(jnp.bfloat16)
    low = (value - high.astype(jnp.float32)).astype(jnp.bfloat16)
    return high, low


def times(left, right):
    left_high, left_low = split(left)
    right_high, right_low = split(right)
    both = jnp.dot(
        jnp.concatenate([left_high, left_low], 0), right_high, preferred_element_type=jnp.float32
    )
    cross = jnp.dot(left_high, right_low, preferred_element_type=jnp.float32)
    return both[:TILE] + (both[TILE:] + cross)


def mask_kernel(density_ref, pattern_ref, out_ref):
    row = 8 * lax.axis_index("x") + 4 * lax.axis_index("c") + lax.axis_index("y")
    layer = lax.axis_index("z")
    for tile in range(2):
        keep = pattern_ref[row, 2 * layer + tile].astype(jnp.float32)
        columns = slice(TILE * tile, TILE * (tile + 1))
        out_ref[:, columns] = density_ref[:, columns] * keep


def mask(density, pattern):
    return pl.pallas_call(
        mask_kernel,
        out_shape=shape(TILE, 2 * TILE),
        in_specs=[VMEM, pl.BlockSpec(memory_space=pltpu.SMEM)],
        out_specs=VMEM,
        compiler_params=pltpu.CompilerParams(vmem_limit_bytes=4 << 20),
    )(density, pattern)


def square_kernel(*refs):
    lefts = refs[:HALF]
    mine_ref, other_ref, own_ref, away_ref, panel_ref = refs[HALF:]
    layer, core = lax.axis_index("z"), lax.axis_index("c")
    pair, parity = lax.div(layer, 2), lax.rem(layer, 2)
    for distance, left_ref in zip(DISTANCES, lefts, strict=True):
        panel_ref[lax.rem(pair + (distance + HALF), HALF)] = left_ref[...]
    own = away = jnp.zeros((TILE, 2 * TILE), jnp.float32)
    for block_ref, half in ((mine_ref, core), (other_ref, 1 - core)):
        for x in range(4):
            left = panel_ref[2 * x + half]
            near = block_ref[pl.ds(4 * x + 2 * parity, 2)].reshape(2 * TILE, 2 * TILE)
            far = block_ref[pl.ds(4 * x + 2 * (1 - parity), 2)].reshape(2 * TILE, 2 * TILE)
            own += times(left, near)
            away += times(left, far)
    own_ref[...] = own
    away_ref[...] = away


def square_call(lefts, mine, other):
    return pl.pallas_call(
        square_kernel,
        out_shape=(shape(TILE, 2 * TILE), shape(TILE, 2 * TILE), shape(HALF, TILE, 2 * TILE)),
        in_specs=[VMEM] * 10,
        out_specs=(VMEM, VMEM, VMEM),
        compiler_params=pltpu.CompilerParams(vmem_limit_bytes=16 << 20),
        cost_estimate=pl.CostEstimate(
            flops=6 * 128 * 2048 * 512, bytes_accessed=6 << 20, transcendentals=0
        ),
    )(*lefts, mine, other)


def cube_kernel(square_ref, here_ref, there_ref, mine_ref, other_ref, out_ref):
    core = lax.axis_index("c")
    parity = lax.rem(lax.axis_index("z"), 2)
    cube = jnp.zeros((TILE, 2 * TILE), jnp.float32)
    for block_ref, half in ((mine_ref, core), (other_ref, 1 - core)):
        for x in range(4):
            for panel_ref, which in ((here_ref, parity), (there_ref, 1 - parity)):
                right = block_ref[pl.ds(4 * x + 2 * which, 2)].reshape(2 * TILE, 2 * TILE)
                cube += times(panel_ref[2 * x + half], right)
    out_ref[...] = 3.0 * square_ref[...] - 2.0 * cube


def cube_call(*operands):
    return pl.pallas_call(
        cube_kernel,
        out_shape=shape(TILE, 2 * TILE),
        in_specs=[VMEM] * 5,
        out_specs=VMEM,
        compiler_params=pltpu.CompilerParams(vmem_limit_bytes=16 << 20),
        cost_estimate=pl.CostEstimate(
            flops=6 * 128 * 4096 * 256, bytes_accessed=6 << 20, transcendentals=0
        ),
    )(*operands)


def ring(block):
    up = [(z, (z + 2) % LAYERS) for z in range(LAYERS)]
    down = [(z, (z - 2) % LAYERS) for z in range(LAYERS)]
    blocks = [block]
    ahead = behind = block
    for _ in range(1, 4):
        ahead = lax.ppermute(ahead, "z", up)
        behind = lax.ppermute(behind, "z", down)
        blocks += [ahead, behind]
    blocks.append(lax.ppermute(ahead, "z", up))
    return blocks


def to_plane(block):
    copies = jnp.broadcast_to(block[None], (16, *block.shape))
    return lax.all_to_all(copies, ("x", "y"), 0, 0)


CORES = [(0, 1), (1, 0)]
NEIGHBOURS = [(z, z ^ 1) for z in range(LAYERS)]
SWAP = [
    (4 * z + y, 4 * (z ^ 1) + (y ^ 2))
    for z in range(LAYERS)
    for y in range(4)
    if z % 2 != y // 2
]


def on_device(density, pattern):
    matched = lax.rem(lax.axis_index("z"), 2) == lax.div(lax.axis_index("y"), 2)
    masked = mask(density, pattern)
    moved = lax.ppermute(masked, ("z", "y"), SWAP)
    lefts = ring(masked)
    mine = to_plane(jnp.where(matched, masked, moved))
    other = lax.ppermute(mine, "c", CORES)
    own, away, here = square_call(lefts, mine, other)
    square = own + lax.ppermute(away, "z", NEIGHBOURS)
    there = lax.ppermute(here, "z", NEIGHBOURS)
    mine = to_plane(square)
    other = lax.ppermute(mine, "c", CORES)
    return cube_call(square, here, there, mine, other)


def solution(mesh):
    split_mesh = Mesh(mesh.devices.reshape(LAYERS, 4, 2, 4), ("z", "x", "c", "y"))
    return jax.shard_map(
        on_device,
        mesh=split_mesh,
        in_specs=(P(("x", "c", "y"), "z"), P()),
        out_specs=P(("x", "c", "y"), "z"),
        check_vma=False,
    )
```

```python
import jax
import jax.numpy as jnp
from jax import lax
from jax.experimental import pallas as pl
from jax.experimental.pallas import tpu as pltpu
from jax.sharding import Mesh
from jax.sharding import PartitionSpec as P


TILE = 128
LAYERS = 16
HALF = 8
DISTANCES = (0, -1, 1, -2, 2, -3, 3, -4)


VMEM = pl.BlockSpec(memory_space=pltpu.VMEM)


def shape(*dims):
    return jax.ShapeDtypeStruct(dims, jnp.float32)


def split(value):
    high = value.astype(jnp.bfloat16)
    low = (value - high.astype(jnp.float32)).astype(jnp.bfloat16)
    return high, low


def times(left, right):
    left_high, left_low = split(left)
    right_high, right_low = split(right)
    both = jnp.dot(
        jnp.concatenate([left_high, left_low], 0), right_high, preferred_element_type=jnp.float32
    )
    cross = jnp.dot(left_high, right_low, preferred_element_type=jnp.float32)
    return both[:TILE] + (both[TILE:] + cross)


def mask_kernel(density_hbm, pattern_hbm, out_ref, density_ref, pattern_ref, sems):
    fetch_pattern = pltpu.make_async_copy(pattern_hbm, pattern_ref, sems.at[0])
    fetch_density = pltpu.make_async_copy(density_hbm, density_ref, sems.at[1])
    fetch_pattern.start()
    fetch_density.start()
    row = 8 * lax.axis_index("x") + 4 * lax.axis_index("c") + lax.axis_index("y")
    layer = lax.axis_index("z")
    fetch_pattern.wait()
    keeps = [pattern_ref[row, 2 * layer + tile].astype(jnp.float32) for tile in range(2)]
    fetch_density.wait()
    for tile in range(2):
        columns = slice(TILE * tile, TILE * (tile + 1))
        out_ref[:, columns] = density_ref[:, columns] * keeps[tile]


def mask(density, pattern):
    hbm = pl.BlockSpec(memory_space=pltpu.HBM)
    return pl.pallas_call(
        mask_kernel,
        out_shape=shape(TILE, 2 * TILE),
        in_specs=[hbm, hbm],
        out_specs=VMEM,
        scratch_shapes=[
            pltpu.VMEM(density.shape, jnp.float32),
            pltpu.SMEM(pattern.shape, jnp.int32),
            pltpu.SemaphoreType.DMA((2,)),
        ],
        compiler_params=pltpu.CompilerParams(vmem_limit_bytes=66_900_000),
    )(density, pattern)


def square_kernel(*refs):
    lefts = refs[:HALF]
    mine_ref, other_ref, own_ref, away_ref, panel_ref = refs[HALF:]
    layer, core = lax.axis_index("z"), lax.axis_index("c")
    pair, parity = lax.div(layer, 2), lax.rem(layer, 2)
    for distance, left_ref in zip(DISTANCES, lefts, strict=True):
        panel_ref[lax.rem(pair + (distance + HALF), HALF)] = left_ref[...]
    own = away = jnp.zeros((TILE, 2 * TILE), jnp.float32)
    for block_ref, half in ((mine_ref, core), (other_ref, 1 - core)):
        for x in range(4):
            left = panel_ref[2 * x + half]
            near = block_ref[pl.ds(4 * x + 2 * parity, 2)].reshape(2 * TILE, 2 * TILE)
            far = block_ref[pl.ds(4 * x + 2 * (1 - parity), 2)].reshape(2 * TILE, 2 * TILE)
            own += times(left, near)
            away += times(left, far)
    own_ref[...] = own
    away_ref[...] = away


def square_call(lefts, mine, other):
    return pl.pallas_call(
        square_kernel,
        out_shape=(shape(TILE, 2 * TILE), shape(TILE, 2 * TILE), shape(HALF, TILE, 2 * TILE)),
        in_specs=[VMEM] * 10,
        out_specs=(VMEM, VMEM, VMEM),
        compiler_params=pltpu.CompilerParams(vmem_limit_bytes=16 << 20),
        cost_estimate=pl.CostEstimate(
            flops=6 * 128 * 2048 * 512, bytes_accessed=6 << 20, transcendentals=0
        ),
    )(*lefts, mine, other)


def cube_kernel(square_ref, here_ref, there_ref, mine_ref, other_ref, out_ref):
    core = lax.axis_index("c")
    parity = lax.rem(lax.axis_index("z"), 2)
    cube = jnp.zeros((TILE, 2 * TILE), jnp.float32)
    for block_ref, half in ((mine_ref, core), (other_ref, 1 - core)):
        for x in range(4):
            for panel_ref, which in ((here_ref, parity), (there_ref, 1 - parity)):
                right = block_ref[pl.ds(4 * x + 2 * which, 2)].reshape(2 * TILE, 2 * TILE)
                cube += times(panel_ref[2 * x + half], right)
    out_ref[...] = 3.0 * square_ref[...] - 2.0 * cube


def cube_call(*operands):
    return pl.pallas_call(
        cube_kernel,
        out_shape=shape(TILE, 2 * TILE),
        in_specs=[VMEM] * 5,
        out_specs=VMEM,
        compiler_params=pltpu.CompilerParams(vmem_limit_bytes=16 << 20),
        cost_estimate=pl.CostEstimate(
            flops=6 * 128 * 4096 * 256, bytes_accessed=6 << 20, transcendentals=0
        ),
    )(*operands)


def ring(block):
    up = [(z, (z + 2) % LAYERS) for z in range(LAYERS)]
    down = [(z, (z - 2) % LAYERS) for z in range(LAYERS)]
    blocks = [block]
    ahead = behind = block
    for _ in range(1, 4):
        ahead = lax.ppermute(ahead, "z", up)
        behind = lax.ppermute(behind, "z", down)
        blocks += [ahead, behind]
    blocks.append(lax.ppermute(ahead, "z", up))
    return blocks


def spread(block):
    return jnp.broadcast_to(block[None], (16, *block.shape))


def to_plane(copies):
    return lax.all_to_all(copies, ("x", "y"), 0, 0)


CORES = [(0, 1), (1, 0)]
NEIGHBOURS = [(z, z ^ 1) for z in range(LAYERS)]
SWAP = [
    (4 * z + y, 4 * (z ^ 1) + (y ^ 2))
    for z in range(LAYERS)
    for y in range(4)
    if z % 2 != y // 2
]


def on_device(density, pattern):
    matched = lax.rem(lax.axis_index("z"), 2) == lax.div(lax.axis_index("y"), 2)
    masked = mask(density, pattern)
    moved = lax.ppermute(masked, ("z", "y"), SWAP)
    lefts = ring(masked)
    mine = to_plane(spread(jnp.where(matched, masked, moved)))
    other = lax.ppermute(mine, "c", CORES)
    own, away, here = square_call(lefts, mine, other)
    square = own + lax.ppermute(away, "z", NEIGHBOURS)
    there = lax.ppermute(here, "z", NEIGHBOURS)
    mine = to_plane(spread(square))
    other = lax.ppermute(mine, "c", CORES)
    return cube_call(square, here, there, mine, other)


def solution(mesh):
    split_mesh = Mesh(mesh.devices.reshape(LAYERS, 4, 2, 4), ("z", "x", "c", "y"))
    return jax.shard_map(
        on_device,
        mesh=split_mesh,
        in_specs=(P(("x", "c", "y"), "z"), P()),
        out_specs=P(("x", "c", "y"), "z"),
        check_vma=False,
    )
```

```python
import functools

import jax
import jax.numpy as jnp
from jax import lax
from jax.experimental import pallas as pl
from jax.experimental.pallas import tpu as pltpu
from jax.sharding import Mesh
from jax.sharding import PartitionSpec as P


TILE = 128
LAYERS = 16
HALF = 8
DISTANCES = (0, -1, 1, -2, 2, -3, 3, -4)


VMEM = pl.BlockSpec(memory_space=pltpu.VMEM)


def shape(*dims):
    return jax.ShapeDtypeStruct(dims, jnp.float32)


def split(value):
    high = value.astype(jnp.bfloat16)
    low = (value - high.astype(jnp.float32)).astype(jnp.bfloat16)
    return high, low


def stack(left):
    high, low = split(left)
    return jnp.concatenate([high, low], 0)


def times(left, right):
    high, low = split(right)
    both = jnp.dot(left, high, preferred_element_type=jnp.float32)
    cross = jnp.dot(left[:TILE], low, preferred_element_type=jnp.float32)
    return both[:TILE] + (both[TILE:] + cross)


def kept(rows_ref, row, layer):
    return rows_ref[pl.ds(row, 1), pl.ds(pl.multiple_of(256 * layer, 256), 256)]


def place():
    layer = lax.axis_index("z")
    return layer, lax.div(layer, 2), lax.rem(layer, 2)


def masked_pair(block_ref, rows_ref, x, half, slot, layer):
    parity = lax.rem(lax.axis_index("z"), 2)
    first = 8 * x + 4 * half + 2 * parity
    return jnp.concatenate(
        [block_ref[4 * x + slot + i] * kept(rows_ref, first + i, layer) for i in range(2)], 0
    )


def near_kernel(*refs):
    lefts = refs[:HALF]
    mine_ref, rows_ref, own_ref, away_ref, panel_ref = refs[HALF:]
    layer, pair, parity = place()
    core = lax.axis_index("c")
    row = 8 * lax.axis_index("x") + 4 * core + lax.axis_index("y")
    for distance, left_ref in zip(DISTANCES, lefts, strict=True):
        slot = lax.rem(pair + (distance + HALF), HALF)
        panel_ref[slot] = left_ref[...] * kept(rows_ref, row, 2 * slot + parity)
    own = away = jnp.zeros((TILE, 2 * TILE), jnp.float32)
    for x in range(4):
        left = stack(panel_ref[2 * x + core])
        own += times(left, masked_pair(mine_ref, rows_ref, x, core, 2 * parity, layer))
        away += times(
            left,
            masked_pair(mine_ref, rows_ref, x, core, 2 - 2 * parity, layer + 1 - 2 * parity),
        )
    own_ref[...] = own
    away_ref[...] = away


def far_kernel(away, panel_ref, other_ref, rows_ref, start_ref, out_ref):
    layer, _, parity = place()
    half = 1 - lax.axis_index("c")
    total = start_ref[...]
    slot = 2 - 2 * parity if away else 2 * parity
    slab = layer + 1 - 2 * parity if away else layer
    for x in range(4):
        right = masked_pair(other_ref, rows_ref, x, half, slot, slab)
        total += times(stack(panel_ref[2 * x + half]), right)
    out_ref[...] = total


def cube_half(here_ref, there_ref, block_ref, half):
    parity = lax.rem(lax.axis_index("z"), 2)
    total = jnp.zeros((TILE, 2 * TILE), jnp.float32)
    for x in range(4):
        for panel_ref, which in ((here_ref, parity), (there_ref, 1 - parity)):
            right = block_ref[pl.ds(4 * x + 2 * which, 2)].reshape(2 * TILE, 2 * TILE)
            total += times(stack(panel_ref[2 * x + half]), right)
    return total


def cube_near_kernel(square_ref, here_ref, there_ref, mine_ref, out_ref):
    cube = cube_half(here_ref, there_ref, mine_ref, lax.axis_index("c"))
    out_ref[...] = 3.0 * square_ref[...] - 2.0 * cube


def cube_far_kernel(start_ref, here_ref, there_ref, other_ref, out_ref):
    cube = cube_half(here_ref, there_ref, other_ref, 1 - lax.axis_index("c"))
    out_ref[...] = start_ref[...] - 2.0 * cube


def call(kernel, out_shape, *operands):
    return pl.pallas_call(
        kernel,
        out_shape=out_shape,
        in_specs=[VMEM] * len(operands),
        out_specs=jax.tree.map(lambda _: VMEM, out_shape),
        compiler_params=pltpu.CompilerParams(vmem_limit_bytes=12 << 20),
        cost_estimate=pl.CostEstimate(
            flops=3 * 128 * 2048 * 512, bytes_accessed=3 << 20, transcendentals=0
        ),
    )(*operands)


def ring(block):
    up = [(z, (z + 2) % LAYERS) for z in range(LAYERS)]
    down = [(z, (z - 2) % LAYERS) for z in range(LAYERS)]
    blocks = [block]
    ahead = behind = block
    for _ in range(1, 4):
        ahead = lax.ppermute(ahead, "z", up)
        behind = lax.ppermute(behind, "z", down)
        blocks += [ahead, behind]
    blocks.append(lax.ppermute(ahead, "z", up))
    return blocks


def spread(block):
    return jnp.broadcast_to(block[None], (16, *block.shape))


def to_plane(copies):
    return lax.all_to_all(copies, ("x", "y"), 0, 0)


CORES = [(0, 1), (1, 0)]
NEIGHBOURS = [(z, z ^ 1) for z in range(LAYERS)]
SWAP = [
    (4 * z + y, 4 * (z ^ 1) + (y ^ 2))
    for z in range(LAYERS)
    for y in range(4)
    if z % 2 != y // 2
]


def on_device(density, pattern):
    block = shape(TILE, 2 * TILE)
    matched = lax.rem(lax.axis_index("z"), 2) == lax.div(lax.axis_index("y"), 2)
    rows = jnp.repeat(pattern.astype(jnp.float32), TILE, axis=1)
    moved = lax.ppermute(density, ("z", "y"), SWAP)
    lefts = ring(density)
    mine = to_plane(spread(jnp.where(matched, density, moved)))
    other = lax.ppermute(mine, "c", CORES)
    own, away, here = call(
        near_kernel, (block, block, shape(HALF, TILE, 2 * TILE)), *lefts, mine, rows
    )
    away = call(functools.partial(far_kernel, True), block, here, other, rows, away)
    own = call(functools.partial(far_kernel, False), block, here, other, rows, own)
    square = own + lax.ppermute(away, "z", NEIGHBOURS)
    there = lax.ppermute(here, "z", NEIGHBOURS)
    mine = to_plane(spread(square))
    other = lax.ppermute(mine, "c", CORES)
    start = call(cube_near_kernel, block, square, here, there, mine)
    return call(cube_far_kernel, block, start, here, there, other)


def solution(mesh):
    split_mesh = Mesh(mesh.devices.reshape(LAYERS, 4, 2, 4), ("z", "x", "c", "y"))
    return jax.shard_map(
        on_device,
        mesh=split_mesh,
        in_specs=(P(("x", "c", "y"), "z"), P()),
        out_specs=P(("x", "c", "y"), "z"),
        check_vma=False,
    )
```

```python
import functools

import jax
import jax.numpy as jnp
from jax import lax
from jax.experimental import pallas as pl
from jax.experimental.pallas import tpu as pltpu
from jax.sharding import Mesh
from jax.sharding import PartitionSpec as P


TILE = 128
LAYERS = 16
HALF = 8
DISTANCES = (0, -1, 1, -2, 2, -3, 3, -4)


VMEM = pl.BlockSpec(memory_space=pltpu.VMEM)


def shape(*dims):
    return jax.ShapeDtypeStruct(dims, jnp.float32)


def split(value):
    high = value.astype(jnp.bfloat16)
    low = (value - high.astype(jnp.float32)).astype(jnp.bfloat16)
    return high, low


def stack(left):
    high, low = split(left)
    return jnp.concatenate([high, low], 0)


def times(left, right):
    high, low = split(right)
    both = jnp.dot(left, high, preferred_element_type=jnp.float32)
    cross = jnp.dot(left[:TILE], low, preferred_element_type=jnp.float32)
    return both[:TILE] + (both[TILE:] + cross)


def kept(rows_ref, row, layer):
    return rows_ref[pl.ds(row, 1), pl.ds(pl.multiple_of(256 * layer, 256), 256)]


def place():
    layer = lax.axis_index("z")
    return layer, lax.div(layer, 2), lax.rem(layer, 2)


def masked_pair(block_ref, rows_ref, x, half, slot, layer):
    parity = lax.rem(lax.axis_index("z"), 2)
    first = 8 * x + 4 * half + 2 * parity
    return jnp.concatenate(
        [block_ref[4 * x + slot + i] * kept(rows_ref, first + i, layer) for i in range(2)], 0
    )


def near_kernel(*refs):
    lefts = refs[:HALF]
    mine_ref, rows_ref, own_ref, away_ref, panel_ref = refs[HALF:]
    layer, pair, parity = place()
    core = lax.axis_index("c")
    row = 8 * lax.axis_index("x") + 4 * core + lax.axis_index("y")
    for distance, left_ref in zip(DISTANCES, lefts, strict=True):
        slot = lax.rem(pair + (distance + HALF), HALF)
        panel_ref[slot] = left_ref[...] * kept(rows_ref, row, 2 * slot + parity)
    own = away = jnp.zeros((TILE, 2 * TILE), jnp.float32)
    for x in range(4):
        left = stack(panel_ref[2 * x + core])
        own += times(left, masked_pair(mine_ref, rows_ref, x, core, 2 * parity, layer))
        away += times(
            left,
            masked_pair(mine_ref, rows_ref, x, core, 2 - 2 * parity, layer + 1 - 2 * parity),
        )
    own_ref[...] = own
    away_ref[...] = away


def far_kernel(away, panel_ref, other_ref, rows_ref, start_ref, out_ref):
    layer, _, parity = place()
    half = 1 - lax.axis_index("c")
    total = start_ref[...]
    slot = 2 - 2 * parity if away else 2 * parity
    slab = layer + 1 - 2 * parity if away else layer
    for x in range(4):
        right = masked_pair(other_ref, rows_ref, x, half, slot, slab)
        total += times(stack(panel_ref[2 * x + half]), right)
    out_ref[...] = total


def cube_half(here_ref, there_ref, block_ref, half):
    parity = lax.rem(lax.axis_index("z"), 2)
    total = jnp.zeros((TILE, 2 * TILE), jnp.float32)
    for x in range(4):
        for panel_ref, which in ((here_ref, parity), (there_ref, 1 - parity)):
            right = block_ref[pl.ds(4 * x + 2 * which, 2)].reshape(2 * TILE, 2 * TILE)
            total += times(stack(panel_ref[2 * x + half]), right)
    return total


def cube_near_kernel(square_ref, here_ref, there_ref, mine_ref, out_ref):
    cube = cube_half(here_ref, there_ref, mine_ref, lax.axis_index("c"))
    out_ref[...] = 3.0 * square_ref[...] - 2.0 * cube


def cube_far_kernel(start_ref, here_ref, there_ref, other_ref, out_ref):
    cube = cube_half(here_ref, there_ref, other_ref, 1 - lax.axis_index("c"))
    out_ref[...] = start_ref[...] - 2.0 * cube


def call(kernel, out_shape, *operands):
    return pl.pallas_call(
        kernel,
        out_shape=out_shape,
        in_specs=[VMEM] * len(operands),
        out_specs=jax.tree.map(lambda _: VMEM, out_shape),
        compiler_params=pltpu.CompilerParams(vmem_limit_bytes=12 << 20),
        cost_estimate=pl.CostEstimate(
            flops=3 * 128 * 2048 * 512, bytes_accessed=3 << 20, transcendentals=0
        ),
    )(*operands)


def ring(block):
    up = [(z, (z + 2) % LAYERS) for z in range(LAYERS)]
    down = [(z, (z - 2) % LAYERS) for z in range(LAYERS)]
    blocks = [block]
    ahead = behind = block
    for _ in range(1, 4):
        ahead = lax.ppermute(ahead, "z", up)
        behind = lax.ppermute(behind, "z", down)
        blocks += [ahead, behind]
    blocks.append(lax.ppermute(ahead, "z", up))
    return blocks


def spread(block):
    return jnp.broadcast_to(block[None], (16, *block.shape))


def to_plane(copies):
    return lax.all_to_all(copies, ("x", "y"), 0, 0)


CORES = [(0, 1), (1, 0)]
NEIGHBOURS = [(z, z ^ 1) for z in range(LAYERS)]
SWAP = [
    (4 * z + y, 4 * z + y if z % 2 == y // 2 else 4 * (z ^ 1) + (y ^ 2))
    for z in range(LAYERS)
    for y in range(4)
]


def on_device(density, pattern):
    block = shape(TILE, 2 * TILE)
    rows = jnp.repeat(pattern.astype(jnp.float32), TILE, axis=1)
    moved = lax.ppermute(density, ("z", "y"), SWAP)
    lefts = ring(density)
    mine = to_plane(spread(moved))
    other = lax.ppermute(mine, "c", CORES)
    own, away, here = call(
        near_kernel, (block, block, shape(HALF, TILE, 2 * TILE)), *lefts, mine, rows
    )
    away = call(functools.partial(far_kernel, True), block, here, other, rows, away)
    own = call(functools.partial(far_kernel, False), block, here, other, rows, own)
    square = own + lax.ppermute(away, "z", NEIGHBOURS)
    there = lax.ppermute(here, "z", NEIGHBOURS)
    mine = to_plane(spread(square))
    other = lax.ppermute(mine, "c", CORES)
    start = call(cube_near_kernel, block, square, here, there, mine)
    return call(cube_far_kernel, block, start, here, there, other)


def solution(mesh):
    split_mesh = Mesh(mesh.devices.reshape(LAYERS, 4, 2, 4), ("z", "x", "c", "y"))
    return jax.shard_map(
        on_device,
        mesh=split_mesh,
        in_specs=(P(("x", "c", "y"), "z"), P()),
        out_specs=P(("x", "c", "y"), "z"),
        check_vma=False,
    )
```
